256 devices in a mesh: grid: 64 (over x_lo, y, z), tm: 4 (over x_hi, core).
Axes of the slice: x: 4 (x_hi: 2, x_lo: 2; x = x_hi * 2 + x_lo), y: 4, z: 8, core: 2. Of those that a mesh axis runs over, the one named last changes fastest.
Arguments:
- temps: float32 [2048, 262144], P('tm', 'grid'), may hold values from -6 to 12
- area_weight: float32 [262144], P('grid'), may hold values from 0.3 to 1
- eofs: bfloat16 [262144, 256], P('grid'), may hold values from -0.03125 to 0.03125
Outputs:
- lag_tiles: float32 [32, 256, 256], P('tm', 'grid')
The draws below stay inside these ranges and needn't reach their ends.
All inputs are finite; a program needn't handle non-finite values.
Results may differ from the reference program's by a relative error of at most 0.0003.
Values sent between devices are 32-bit elements; how exact they have to be, the bound alone decides.
No kernel may reach another device: no remote copies, remote signals or barrier semaphores. Data moves between devices by JAX's collectives and lax.ppermute only.
A program may use at most 64 MiB of HBM per device.

```python
import jax
import jax.numpy as jnp
from jax import lax

COLS_DEV = 4096
K = 256
LAGS = 32
HOURS = 2048
COLS = 262144
N_GRID = 64


def draw_temps(key, part):
    key_level = jax.random.fold_in(key, 11)
    key_jitter = jax.random.fold_in(key, 12)
    growth = 0.25 + 1.75 * (jnp.arange(HOURS, dtype=jnp.float32)[:, None] / HOURS)
    levels = jax.random.uniform(key_level, (1, COLS), jnp.float32, 1.0, 2.0)
    jitter = jnp.clip(jax.random.normal(key_jitter, (HOURS, COLS), jnp.float32), -6.0, 6.0)
    return levels * growth + jitter


def strengthened(entries, stream_key, source, target, blocks, factor):
    def block_of(dim):
        return (jnp.arange(entries.shape[dim]) // (entries.shape[dim] // blocks)).reshape((-1,) + (1,) * (entries.ndim - 1 - dim))

    one_side = jax.random.permutation(stream_key, blocks)[block_of(target)]
    second = (block_of(target) + blocks // 2) % blocks
    return jnp.where((block_of(source) == one_side) | (block_of(source) == second), factor * entries, entries)


def steps_of(own_key, extent, cuts, least, top_value):
    gain, own = 1.0, jax.random.fold_in(own_key, 6)
    for position, shards_of in cuts:
        heights = jnp.exp(jax.random.uniform(jax.random.fold_in(own, position), (shards_of,), jnp.float32, least / len(cuts), top_value / len(cuts)))
        gain = gain * jnp.repeat(heights, extent[position] // shards_of).reshape([-1 if axis == position else 1 for axis in range(len(extent))])
    return gain


def gaussian_with(stream_key, dims, scale, most, cuts, heavy, kind=jnp.bfloat16):
    values = scale * jax.random.normal(stream_key, dims, jnp.float32)
    if cuts:
        values = values * steps_of(stream_key, dims, cuts, -0.22, 0.18)
    return jnp.clip(strengthened(values, jax.random.fold_in(stream_key, 3), *heavy), -most, most).astype(kind)


def setup_inputs(seed: int = 0) -> dict:
    keys = jax.random.split(jax.random.key(seed), 4)
    return {
        "temps": draw_temps(jax.random.fold_in(keys[3], 71), 0),
        "area_weight": jnp.clip(0.3 + 0.7 * jax.random.uniform(keys[1], (COLS,), jnp.float32) ** steps_of(keys[1], (COLS,), ((0, 64),), -0.2, 0.2), 0.3, 1.0),
        "eofs": gaussian_with(keys[2], (COLS, K), COLS ** -0.5, 0.03125, ((0, 64),), (0, 1, 64, 4.0)),
    }


def reference(temps, area_weight, eofs):
    column_mean = jnp.sum(temps, axis=0) / HOURS

    def add_block(block_index, total):
        begin = (block_index * COLS_DEV).astype(jnp.int32)
        temp_block = lax.dynamic_slice_in_dim(temps, begin, COLS_DEV, 1)
        mean_block = lax.dynamic_slice_in_dim(column_mean, begin, COLS_DEV, 0)
        weight_block = lax.dynamic_slice_in_dim(area_weight, begin, COLS_DEV, 0)
        eof_block = lax.dynamic_slice_in_dim(eofs, begin, COLS_DEV, 0)
        anomaly = ((temp_block - mean_block) * weight_block).astype(jnp.bfloat16)
        return total + jnp.dot(anomaly, eof_block, preferred_element_type=jnp.float32)

    components = lax.fori_loop(0, N_GRID, add_block, jnp.zeros((HOURS, K), jnp.float32))
    padded = jnp.concatenate([components, jnp.zeros((LAGS - 1, K), jnp.float32)], axis=0)

    def one_lag(lag_index):
        shifted = lax.dynamic_slice_in_dim(padded, lag_index, HOURS, 0)
        return jnp.dot(components.T, shifted, precision=lax.Precision.HIGHEST) / HOURS

    return lax.map(one_lag, jnp.arange(LAGS, dtype=jnp.int32))
```

```python
import jax
import jax.numpy as jnp
from jax import lax
from jax.experimental import pallas as pl
from jax.experimental.pallas import tpu as pltpu
from jax.sharding import Mesh, PartitionSpec as P

AXES = ("xl", "y", "z", "xh", "core")
SIZES = (2, 4, 8, 2, 2)
COL_BLOCK = 512
HOURS = 2048
HOURS_DEV = 512
CHANNELS = 256
LAGS_DEV = 8
TILE = 32
VMEM_SPEC = pl.BlockSpec(memory_space=pltpu.VMEM)
SMEM_SPEC = pl.BlockSpec(memory_space=pltpu.SMEM)


def project_kernel(temps_ref, weight_ref, eofs_ref, out_ref, acc_ref, mean_ref):
    step = pl.program_id(0)

    @pl.when(step == 0)
    def _():
        acc_ref[...] = jnp.zeros_like(acc_ref)
        mean_ref[...] = jnp.zeros_like(mean_ref)

    temps = temps_ref[...]
    weight = weight_ref[...]
    eofs = eofs_ref[...]
    block_mean = jnp.sum(temps, axis=0, keepdims=True) * (1.0 / HOURS_DEV)
    anomaly = (temps - block_mean) * weight
    high = anomaly.astype(jnp.bfloat16)
    low = (anomaly - high.astype(jnp.float32)).astype(jnp.bfloat16)
    acc_ref[...] += jnp.dot(high, eofs, preferred_element_type=jnp.float32) + jnp.dot(
        low, eofs, preferred_element_type=jnp.float32
    )
    level = block_mean * weight
    first = level.astype(jnp.bfloat16).astype(jnp.float32)
    second = (level - first).astype(jnp.bfloat16).astype(jnp.float32)
    third = level - first - second
    row = lax.broadcasted_iota(jnp.int32, (16, level.shape[1]), 0)
    terms = jnp.where(row == 0, first, jnp.where(row == 1, second, jnp.where(row == 2, third, 0.0)))
    mean_ref[...] += jnp.dot(terms.astype(jnp.bfloat16), eofs, preferred_element_type=jnp.float32)

    @pl.when(step == pl.num_programs(0) - 1)
    def _():
        offset = jnp.sum(mean_ref[...], axis=0, keepdims=True)
        out_ref[...] = (acc_ref[...] + offset).T


def project(temps, area_weight, eofs):
    cols = temps.shape[1]
    return pl.pallas_call(
        project_kernel,
        grid=(cols // COL_BLOCK,),
        in_specs=[
            pl.BlockSpec((HOURS_DEV, COL_BLOCK), lambda k: (0, k)),
            pl.BlockSpec((1, COL_BLOCK), lambda k: (0, k)),
            pl.BlockSpec((COL_BLOCK, CHANNELS), lambda k: (k, 0)),
        ],
        out_specs=pl.BlockSpec((CHANNELS, HOURS_DEV), lambda k: (0, 0)),
        out_shape=jax.ShapeDtypeStruct((CHANNELS, HOURS_DEV), jnp.float32),
        scratch_shapes=[
            pltpu.VMEM((HOURS_DEV, CHANNELS), jnp.float32),
            pltpu.VMEM((16, CHANNELS), jnp.float32),
        ],
        compiler_params=pltpu.CompilerParams(dimension_semantics=("arbitrary",)),
        name="project",
    )(temps, area_weight.reshape(1, cols), eofs)


def sum_rows_kernel(parts_ref, out_ref):
    total = jnp.sum(parts_ref[...], axis=0)
    for owner in range(8):
        for seg in range(4):
            out_ref[owner, seg * 4 : seg * 4 + 4, :] = total[owner * 4 : owner * 4 + 4, seg * 128 : seg * 128 + 128]


def sum_rows(parts):
    return pl.pallas_call(
        sum_rows_kernel,
        in_specs=[VMEM_SPEC],
        out_specs=VMEM_SPEC,
        out_shape=jax.ShapeDtypeStruct((8, 16, 128), jnp.float32),
        name="sum_rows",
    )(parts)


def place(block, dest_ref):
    for source in range(16):
        chan, half = source // 2, source % 2
        for core in range(2):
            for seg in range(4):
                row = core * 16 + seg * 4
                hour = ((half * 2 + core) * 4 + seg) * 128
                dest_ref[chan * 4 : chan * 4 + 4, hour : hour + 128] = block[source, row : row + 4, :]


def tiles_kernel(where_ref, mine_ref, other_ref, out_ref, a_ref, b_ref, shifted_ref):
    core = where_ref[0]
    first_lag = where_ref[1]
    mine = mine_ref[...]
    other = other_ref[...]
    place(jnp.where(core == 0, mine, other), a_ref)
    place(jnp.where(core == 0, other, mine), b_ref)
    a = a_ref[...]
    a = a - jnp.sum(a, axis=1, keepdims=True) * (1.0 / HOURS)
    b = b_ref[:, :HOURS]
    b_ref[:, :HOURS] = b - jnp.sum(b, axis=1, keepdims=True) * (1.0 / HOURS)
    b_ref[:, HOURS:] = jnp.zeros((TILE, 128), jnp.float32)
    width = HOURS + 128
    ext = pltpu.roll(b_ref[...], jnp.where(first_lag == 0, 0, width - first_lag), 1)
    for lag in range(LAGS_DEV):
        if lag:
            ext = pltpu.roll(ext, width - 1, 1)
        shifted_ref[lag * TILE : (lag + 1) * TILE, :] = ext[:, :HOURS]
    tile = lax.dot_general(
        a,
        shifted_ref[...],
        (((1,), (1,)), ((), ())),
        precision=lax.Precision.HIGHEST,
        preferred_element_type=jnp.float32,
    ) * (1.0 / HOURS)
    for owner in range(8):
        for half in range(2):
            out_ref[owner, half * 4 : half * 4 + 4, :] = tile[owner * 4 : owner * 4 + 4, half * 128 : half * 128 + 128]


def tiles(where, mine, other):
    return pl.pallas_call(
        tiles_kernel,
        in_specs=[SMEM_SPEC, VMEM_SPEC, VMEM_SPEC],
        out_specs=VMEM_SPEC,
        out_shape=jax.ShapeDtypeStruct((8, 8, 128), jnp.float32),
        scratch_shapes=[
            pltpu.VMEM((TILE, HOURS), jnp.float32),
            pltpu.VMEM((TILE, HOURS + 128), jnp.float32),
            pltpu.VMEM((LAGS_DEV * TILE, HOURS), jnp.float32),
        ],
        name="tiles",
    )(where, mine, other)


def spread_kernel(parts_ref, out_ref):
    for lag in range(LAGS_DEV):
        row, lane = 4 * (lag // 4), TILE * (lag % 4)
        for source in range(8):
            out_ref[lag, :, source * TILE : (source + 1) * TILE] = parts_ref[source, row : row + 4, lane : lane + TILE]


def spread(parts):
    return pl.pallas_call(
        spread_kernel,
        in_specs=[VMEM_SPEC],
        out_specs=VMEM_SPEC,
        out_shape=jax.ShapeDtypeStruct((LAGS_DEV, 4, CHANNELS), jnp.float32),
        name="spread",
    )(parts)


def device(i, z, xh, core):
    return ((i * 8 + z) * 2 + xh) * 2 + core


GATHER_GROUPS = [[device(i, z, xh, 0) for i in range(8) for xh in range(2)] for z in range(8)] + [
    [device(i, z, xh, 1) for z in range(8) for xh in range(2)] for i in range(8)
]
SWAP = [(0, 1), (1, 0)]


def shards(temps, area_weight, eofs):
    partial_sums = project(temps, area_weight, eofs)
    parts = lax.all_to_all(partial_sums.reshape(8, TILE, HOURS_DEV), ("xl", "y"), 0, 0)
    parts = lax.all_to_all(sum_rows(parts), "z", 0, 0)
    piece = jnp.sum(parts, axis=0)
    core = lax.axis_index("core")
    neighbour = lax.ppermute(piece, "core", SWAP)
    pair = jnp.where(
        core == 0,
        jnp.concatenate([piece, neighbour], axis=0),
        jnp.concatenate([neighbour, piece], axis=0),
    )
    mine = lax.all_to_all(
        jnp.broadcast_to(pair[None], (16, 32, 128)), AXES, 0, 0, axis_index_groups=GATHER_GROUPS
    )
    other = lax.ppermute(mine, "core", SWAP)
    first_lag = (lax.axis_index("xh") * 2 + core) * LAGS_DEV
    where = jnp.stack([core, first_lag]).astype(jnp.int32)
    out = lax.all_to_all(tiles(where, mine, other), ("xl", "y"), 0, 0)
    return spread(out)


def solution(mesh):
    fine = Mesh(mesh.devices.reshape(SIZES), AXES)
    grid, tm = ("xl", "y", "z"), ("xh", "core")
    return jax.shard_map(
        shards,
        mesh=fine,
        in_specs=(P(tm, grid), P(grid), P(grid, None)),
        out_specs=P(tm, grid, None),
        check_vma=False,
    )
```

```python
import jax
import jax.numpy as jnp
from jax import lax
from jax.experimental import pallas as pl
from jax.experimental.pallas import tpu as pltpu
from jax.sharding import Mesh, PartitionSpec as P

AXES = ("xl", "y", "z", "xh", "core")
SIZES = (2, 4, 8, 2, 2)
COL_BLOCK = 512
ROW_BLOCK = 256
COPIES_AHEAD = 4
HOURS = 2048
HOURS_DEV = 512
CHANNELS = 256
LAGS_DEV = 8
TILE = 32
VMEM_SPEC = pl.BlockSpec(memory_space=pltpu.VMEM)
ANY_SPEC = pl.BlockSpec(memory_space=pl.ANY)


def on_chip(x):
    return pltpu.with_memory_space_constraint(x, pltpu.VMEM)


def project_kernel(temps_hbm, weight_hbm, eofs_hbm, out_ref, temps, weight, eofs, acc_ref, temps_sem, eofs_sem, weight_sem):
    blocks = temps.shape[0]
    weight_copy = pltpu.make_async_copy(weight_hbm, weight, weight_sem)
    weight_copy.start()
    temps_copies = [
        pltpu.make_async_copy(temps_hbm.at[:, pl.ds(k * COL_BLOCK, COL_BLOCK)], temps.at[k], temps_sem.at[k])
        for k in range(blocks)
    ]
    eofs_copies = [
        pltpu.make_async_copy(eofs_hbm.at[pl.ds(k * COL_BLOCK, COL_BLOCK), :], eofs.at[k], eofs_sem.at[k])
        for k in range(blocks)
    ]
    for k in range(COPIES_AHEAD):
        temps_copies[k].start()
        eofs_copies[k].start()
    weight_copy.wait()
    for k in range(blocks):
        temps_copies[k].wait()
        eofs_copies[k].wait()
        if k + COPIES_AHEAD < blocks:
            temps_copies[k + COPIES_AHEAD].start()
            eofs_copies[k + COPIES_AHEAD].start()
        first = k * (COL_BLOCK // 128)
        column_weight = jnp.concatenate(
            [weight[first + j : first + j + 1, :] for j in range(COL_BLOCK // 128)], axis=1
        )
        for row in range(0, HOURS_DEV, ROW_BLOCK):
            rows = slice(row, row + ROW_BLOCK)
            weighted = temps[k, rows, :] * column_weight
            high = weighted.astype(jnp.bfloat16)
            low = (weighted - high.astype(jnp.float32)).astype(jnp.bfloat16)
            product = jnp.dot(high, eofs[k], preferred_element_type=jnp.float32) + jnp.dot(
                low, eofs[k], preferred_element_type=jnp.float32
            )
            if k:
                acc_ref[rows, :] += product
            else:
                acc_ref[rows, :] = product
    out_ref[...] = acc_ref[...].T


def project(temps, area_weight, eofs):
    cols = temps.shape[1]
    blocks = cols // COL_BLOCK
    return pl.pallas_call(
        project_kernel,
        in_specs=[ANY_SPEC, ANY_SPEC, ANY_SPEC],
        out_specs=VMEM_SPEC,
        out_shape=pltpu.VMEM((CHANNELS, HOURS_DEV), jnp.float32),
        scratch_shapes=[
            pltpu.VMEM((blocks, HOURS_DEV, COL_BLOCK), jnp.float32),
            pltpu.VMEM((cols // 128, 128), jnp.float32),
            pltpu.VMEM((blocks, COL_BLOCK, CHANNELS), jnp.bfloat16),
            pltpu.VMEM((HOURS_DEV, CHANNELS), jnp.float32),
            pltpu.SemaphoreType.DMA((blocks,)),
            pltpu.SemaphoreType.DMA((blocks,)),
            pltpu.SemaphoreType.DMA(()),
        ],
        name="project",
    )(temps, area_weight.reshape(cols // 128, 128), eofs)


def sum_rows_kernel(parts_ref, out_ref):
    total = jnp.sum(parts_ref[...], axis=0)
    for owner in range(8):
        for seg in range(4):
            out_ref[owner, seg * 4 : seg * 4 + 4, :] = total[owner * 4 : owner * 4 + 4, seg * 128 : seg * 128 + 128]


def sum_rows(parts):
    return pl.pallas_call(
        sum_rows_kernel,
        in_specs=[VMEM_SPEC],
        out_specs=VMEM_SPEC,
        out_shape=pltpu.VMEM((8, 16, 128), jnp.float32),
        name="sum_rows",
    )(on_chip(parts))


def place(block, dest_ref):
    for source in range(16):
        chan, half = source // 2, source % 2
        for core in range(2):
            for seg in range(4):
                row = core * 16 + seg * 4
                hour = ((half * 2 + core) * 4 + seg) * 128
                dest_ref[chan * 4 : chan * 4 + 4, hour : hour + 128] = block[source, row : row + 4, :]


def tiles_kernel(mine_ref, other_ref, out_ref, a_ref, b_ref, shifted_ref):
    core = lax.axis_index("core")
    first_lag = (lax.axis_index("xh") * 2 + core) * LAGS_DEV
    mine = mine_ref[...]
    other = other_ref[...]
    place(jnp.where(core == 0, mine, other), a_ref)
    place(jnp.where(core == 0, other, mine), b_ref)
    a = a_ref[...]
    a = a - jnp.sum(a, axis=1, keepdims=True) * (1.0 / HOURS)
    b = b_ref[:, :HOURS]
    b_ref[:, :HOURS] = b - jnp.sum(b, axis=1, keepdims=True) * (1.0 / HOURS)
    b_ref[:, HOURS:] = jnp.zeros((TILE, 128), jnp.float32)
    width = HOURS + 128
    ext = pltpu.roll(b_ref[...], jnp.where(first_lag == 0, 0, width - first_lag), 1)
    for lag in range(LAGS_DEV):
        if lag:
            ext = pltpu.roll(ext, width - 1, 1)
        shifted_ref[lag * TILE : (lag + 1) * TILE, :] = ext[:, :HOURS]
    tile = lax.dot_general(
        a,
        shifted_ref[...],
        (((1,), (1,)), ((), ())),
        precision=lax.Precision.HIGHEST,
        preferred_element_type=jnp.float32,
    ) * (1.0 / HOURS)
    for owner in range(8):
        for half in range(2):
            out_ref[owner, half * 4 : half * 4 + 4, :] = tile[owner * 4 : owner * 4 + 4, half * 128 : half * 128 + 128]


def tiles(mine, other):
    return pl.pallas_call(
        tiles_kernel,
        in_specs=[VMEM_SPEC, VMEM_SPEC],
        out_specs=VMEM_SPEC,
        out_shape=pltpu.VMEM((8, 8, 128), jnp.float32),
        scratch_shapes=[
            pltpu.VMEM((TILE, HOURS), jnp.float32),
            pltpu.VMEM((TILE, HOURS + 128), jnp.float32),
            pltpu.VMEM((LAGS_DEV * TILE, HOURS), jnp.float32),
        ],
        name="tiles",
    )(on_chip(mine), on_chip(other))


def spread_kernel(parts_ref, out_ref):
    for lag in range(LAGS_DEV):
        row, lane = 4 * (lag // 4), TILE * (lag % 4)
        for source in range(8):
            out_ref[lag, :, source * TILE : (source + 1) * TILE] = parts_ref[source, row : row + 4, lane : lane + TILE]


def spread(parts):
    return pl.pallas_call(
        spread_kernel,
        in_specs=[VMEM_SPEC],
        out_specs=VMEM_SPEC,
        out_shape=jax.ShapeDtypeStruct((LAGS_DEV, 4, CHANNELS), jnp.float32),
        name="spread",
    )(on_chip(parts))


def device(i, z, xh, core):
    return ((i * 8 + z) * 2 + xh) * 2 + core


GATHER_GROUPS = [[device(i, z, xh, 0) for i in range(8) for xh in range(2)] for z in range(8)] + [
    [device(i, z, xh, 1) for z in range(8) for xh in range(2)] for i in range(8)
]
SWAP = [(0, 1), (1, 0)]


def shards(temps, area_weight, eofs):
    partial_sums = project(temps, area_weight, eofs)
    parts = lax.all_to_all(partial_sums.reshape(8, TILE, HOURS_DEV), ("xl", "y"), 0, 0)
    parts = lax.all_to_all(sum_rows(parts), "z", 0, 0)
    piece = jnp.sum(parts, axis=0)
    core = lax.axis_index("core")
    neighbour = lax.ppermute(piece, "core", SWAP)
    pair = jnp.where(
        core == 0,
        jnp.concatenate([piece, neighbour], axis=0),
        jnp.concatenate([neighbour, piece], axis=0),
    )
    mine = lax.all_to_all(
        jnp.broadcast_to(pair[None], (16, 32, 128)), AXES, 0, 0, axis_index_groups=GATHER_GROUPS
    )
    other = lax.ppermute(mine, "core", SWAP)
    out = lax.all_to_all(tiles(mine, other), ("xl", "y"), 0, 0)
    return spread(out)


def solution(mesh):
    fine = Mesh(mesh.devices.reshape(SIZES), AXES)
    grid, tm = ("xl", "y", "z"), ("xh", "core")
    return jax.shard_map(
        shards,
        mesh=fine,
        in_specs=(P(tm, grid), P(grid), P(grid, None)),
        out_specs=P(tm, grid, None),
        check_vma=False,
    )
```

```python
import jax
import jax.numpy as jnp
from jax import lax
from jax.experimental import pallas as pl
from jax.experimental.pallas import tpu as pltpu
from jax.sharding import Mesh, PartitionSpec as P

AXES = ("xl", "y", "z", "xh", "core")
SIZES = (2, 4, 8, 2, 2)
COL_BLOCK = 512
ROW_BLOCK = 256
COPIES_AHEAD = 4
HOURS = 2048
HOURS_DEV = 512
CHANNELS = 256
LAGS_DEV = 8
TILE = 32
VMEM_SPEC = pl.BlockSpec(memory_space=pltpu.VMEM)
ANY_SPEC = pl.BlockSpec(memory_space=pl.ANY)


def on_chip(x):
    return pltpu.with_memory_space_constraint(x, pltpu.VMEM)


def project_kernel(temps_hbm, weight_hbm, eofs_hbm, out_ref, temps, weight, eofs, acc_ref, temps_sem, eofs_sem, weight_sem):
    blocks = temps.shape[0]
    weight_copy = pltpu.make_async_copy(weight_hbm, weight, weight_sem)
    weight_copy.start()
    temps_copies = [
        pltpu.make_async_copy(temps_hbm.at[:, pl.ds(k * COL_BLOCK, COL_BLOCK)], temps.at[k], temps_sem.at[k])
        for k in range(blocks)
    ]
    eofs_copies = [
        pltpu.make_async_copy(eofs_hbm.at[pl.ds(k * COL_BLOCK, COL_BLOCK), :], eofs.at[k], eofs_sem.at[k])
        for k in range(blocks)
    ]
    for k in range(COPIES_AHEAD):
        temps_copies[k].start()
        eofs_copies[k].start()
    weight_copy.wait()
    for k in range(blocks):
        temps_copies[k].wait()
        eofs_copies[k].wait()
        if k + COPIES_AHEAD < blocks:
            temps_copies[k + COPIES_AHEAD].start()
            eofs_copies[k + COPIES_AHEAD].start()
        first = k * (COL_BLOCK // 128)
        column_weight = jnp.concatenate(
            [weight[first + j : first + j + 1, :] for j in range(COL_BLOCK // 128)], axis=1
        )
        for row in range(0, HOURS_DEV, ROW_BLOCK):
            rows = slice(row, row + ROW_BLOCK)
            weighted = temps[k, rows, :] * column_weight
            high = weighted.astype(jnp.bfloat16)
            low = (weighted - high.astype(jnp.float32)).astype(jnp.bfloat16)
            product = jnp.dot(high, eofs[k], preferred_element_type=jnp.float32) + jnp.dot(
                low, eofs[k], preferred_element_type=jnp.float32
            )
            if k:
                acc_ref[rows, :] += product
            else:
                acc_ref[rows, :] = product
    out_ref[...] = acc_ref[...].T


def project(temps, area_weight, eofs):
    cols = temps.shape[1]
    blocks = cols // COL_BLOCK
    return pl.pallas_call(
        project_kernel,
        in_specs=[ANY_SPEC, ANY_SPEC, ANY_SPEC],
        out_specs=VMEM_SPEC,
        out_shape=pltpu.VMEM((CHANNELS, HOURS_DEV), jnp.float32),
        scratch_shapes=[
            pltpu.VMEM((blocks, HOURS_DEV, COL_BLOCK), jnp.float32),
            pltpu.VMEM((cols // 128, 128), jnp.float32),
            pltpu.VMEM((blocks, COL_BLOCK, CHANNELS), jnp.bfloat16),
            pltpu.VMEM((HOURS_DEV, CHANNELS), jnp.float32),
            pltpu.SemaphoreType.DMA((blocks,)),
            pltpu.SemaphoreType.DMA((blocks,)),
            pltpu.SemaphoreType.DMA(()),
        ],
        name="project",
    )(temps, area_weight.reshape(cols // 128, 128), eofs)


def sum_rows_kernel(parts_ref, out_ref):
    total = jnp.sum(parts_ref[...], axis=0)
    for owner in range(8):
        for seg in range(4):
            out_ref[owner, seg * 4 : seg * 4 + 4, :] = total[owner * 4 : owner * 4 + 4, seg * 128 : seg * 128 + 128]


def sum_rows(parts):
    return pl.pallas_call(
        sum_rows_kernel,
        in_specs=[VMEM_SPEC],
        out_specs=VMEM_SPEC,
        out_shape=pltpu.VMEM((8, 16, 128), jnp.float32),
        name="sum_rows",
    )(on_chip(parts))


def place(block, dest_ref):
    for source in range(16):
        chan, half = source // 2, source % 2
        for core in range(2):
            for seg in range(4):
                row = core * 16 + seg * 4
                hour = ((half * 2 + core) * 4 + seg) * 128
                dest_ref[chan * 4 : chan * 4 + 4, hour : hour + 128] = block[source, row : row + 4, :]


def split(x):
    high = x.astype(jnp.bfloat16)
    return high, (x - high.astype(jnp.float32)).astype(jnp.bfloat16)


def tiles_kernel(mine_ref, other_ref, out_ref, a_ref, b_ref, shifted_ref):
    core = lax.axis_index("core")
    first_lag = (lax.axis_index("xh") * 2 + core) * LAGS_DEV
    mine = mine_ref[...]
    other = other_ref[...]
    place(jnp.where(core == 0, mine, other), a_ref)
    place(jnp.where(core == 0, other, mine), b_ref)
    a = a_ref[...]
    a = a - jnp.sum(a, axis=1, keepdims=True) * (1.0 / HOURS)
    b = b_ref[:, :HOURS]
    b_ref[:, :HOURS] = b - jnp.sum(b, axis=1, keepdims=True) * (1.0 / HOURS)
    b_ref[:, HOURS:] = jnp.zeros((TILE, 128), jnp.float32)
    width = HOURS + 128
    ext = pltpu.roll(b_ref[...], jnp.where(first_lag == 0, 0, width - first_lag), 1)
    half = LAGS_DEV // 2
    late = jnp.where(lax.broadcasted_iota(jnp.int32, a.shape, 1) < half, 0.0, pltpu.roll(a, half, 1))
    left = jnp.concatenate([*split(a), *split(late)], axis=0)
    for lag in range(half):
        moved = (pltpu.roll(ext, width - lag, 1) if lag else ext)[:, :HOURS]
        high, low = split(moved)
        shifted_ref[lag * TILE : (lag + 1) * TILE, :] = high
        shifted_ref[128 + lag * TILE : 128 + (lag + 1) * TILE, :] = low
    product = lax.dot_general(
        left, shifted_ref[...], (((1,), (1,)), ((), ())), preferred_element_type=jnp.float32
    )
    for p in range(2):
        high, low = product[2 * p * TILE : (2 * p + 1) * TILE, :], product[(2 * p + 1) * TILE : (2 * p + 2) * TILE, :]
        tile = (high[:, :128] + low[:, :128] + high[:, 128:]) * (1.0 / HOURS)
        for owner in range(8):
            out_ref[owner, p * 4 : p * 4 + 4, :] = tile[owner * 4 : owner * 4 + 4, :]


def tiles(mine, other):
    return pl.pallas_call(
        tiles_kernel,
        in_specs=[VMEM_SPEC, VMEM_SPEC],
        out_specs=VMEM_SPEC,
        out_shape=pltpu.VMEM((8, 8, 128), jnp.float32),
        scratch_shapes=[
            pltpu.VMEM((TILE, HOURS), jnp.float32),
            pltpu.VMEM((TILE, HOURS + 128), jnp.float32),
            pltpu.VMEM((LAGS_DEV * TILE, HOURS), jnp.bfloat16),
        ],
        name="tiles",
    )(on_chip(mine), on_chip(other))


def spread_kernel(parts_ref, out_ref):
    for lag in range(LAGS_DEV):
        row, lane = 4 * (lag // 4), TILE * (lag % 4)
        for source in range(8):
            out_ref[lag, :, source * TILE : (source + 1) * TILE] = parts_ref[source, row : row + 4, lane : lane + TILE]


def spread(parts):
    return pl.pallas_call(
        spread_kernel,
        in_specs=[VMEM_SPEC],
        out_specs=VMEM_SPEC,
        out_shape=jax.ShapeDtypeStruct((LAGS_DEV, 4, CHANNELS), jnp.float32),
        name="spread",
    )(on_chip(parts))


def device(i, z, xh, core):
    return ((i * 8 + z) * 2 + xh) * 2 + core


GATHER_GROUPS = [[device(i, z, xh, 0) for i in range(8) for xh in range(2)] for z in range(8)] + [
    [device(i, z, xh, 1) for z in range(8) for xh in range(2)] for i in range(8)
]
SWAP = [(0, 1), (1, 0)]


def shards(temps, area_weight, eofs):
    partial_sums = project(temps, area_weight, eofs)
    parts = lax.all_to_all(partial_sums.reshape(8, TILE, HOURS_DEV), ("xl", "y"), 0, 0)
    parts = lax.all_to_all(sum_rows(parts), "z", 0, 0)
    piece = jnp.sum(parts, axis=0)
    core = lax.axis_index("core")
    neighbour = lax.ppermute(piece, "core", SWAP)
    pair = jnp.where(
        core == 0,
        jnp.concatenate([piece, neighbour], axis=0),
        jnp.concatenate([neighbour, piece], axis=0),
    )
    mine = lax.all_to_all(
        jnp.broadcast_to(pair[None], (16, 32, 128)), AXES, 0, 0, axis_index_groups=GATHER_GROUPS
    )
    other = lax.ppermute(mine, "core", SWAP)
    out = lax.all_to_all(tiles(mine, other), ("xl", "y"), 0, 0)
    return spread(out)


def solution(mesh):
    fine = Mesh(mesh.devices.reshape(SIZES), AXES)
    grid, tm = ("xl", "y", "z"), ("xh", "core")
    return jax.shard_map(
        shards,
        mesh=fine,
        in_specs=(P(tm, grid), P(grid), P(grid, None)),
        out_specs=P(tm, grid, None),
        check_vma=False,
    )
```

```python
import jax
import jax.numpy as jnp
from jax import lax
from jax.experimental import pallas as pl
from jax.experimental.pallas import tpu as pltpu
from jax.sharding import Mesh, PartitionSpec as P

AXES = ("xl", "y", "z", "xh", "core")
SIZES = (2, 4, 8, 2, 2)
COL_BLOCK = 512
ROW_BLOCK = 256
COPIES_AHEAD = 4
HOURS = 2048
HOURS_DEV = 512
CHANNELS = 256
LAGS_DEV = 8
TILE = 32
VMEM_SPEC = pl.BlockSpec(memory_space=pltpu.VMEM)
ANY_SPEC = pl.BlockSpec(memory_space=pl.ANY)


def on_chip(x):
    return pltpu.with_memory_space_constraint(x, pltpu.VMEM)


def project_kernel(temps_hbm, weight_hbm, eofs_hbm, out_ref, temps, weight, eofs, acc_ref, temps_sem, eofs_sem, weight_sem):
    blocks = temps.shape[0]
    weight_copy = pltpu.make_async_copy(weight_hbm, weight, weight_sem)
    weight_copy.start()
    temps_copies = [
        pltpu.make_async_copy(temps_hbm.at[:, pl.ds(k * COL_BLOCK, COL_BLOCK)], temps.at[k], temps_sem.at[k])
        for k in range(blocks)
    ]
    eofs_copies = [
        pltpu.make_async_copy(eofs_hbm.at[pl.ds(k * COL_BLOCK, COL_BLOCK), :], eofs.at[k], eofs_sem.at[k])
        for k in range(blocks)
    ]
    for k in range(COPIES_AHEAD):
        temps_copies[k].start()
        eofs_copies[k].start()
    weight_copy.wait()
    for k in range(blocks):
        temps_copies[k].wait()
        eofs_copies[k].wait()
        if k + COPIES_AHEAD < blocks:
            temps_copies[k + COPIES_AHEAD].start()
            eofs_copies[k + COPIES_AHEAD].start()
        first = k * (COL_BLOCK // 128)
        column_weight = jnp.concatenate(
            [weight[first + j : first + j + 1, :] for j in range(COL_BLOCK // 128)], axis=1
        )
        for row in range(0, HOURS_DEV, ROW_BLOCK):
            rows = slice(row, row + ROW_BLOCK)
            weighted = temps[k, rows, :] * column_weight
            high = weighted.astype(jnp.bfloat16)
            low = (weighted - high.astype(jnp.float32)).astype(jnp.bfloat16)
            product = jnp.dot(high, eofs[k], preferred_element_type=jnp.float32) + jnp.dot(
                low, eofs[k], preferred_element_type=jnp.float32
            )
            if k:
                acc_ref[rows, :] += product
            else:
                acc_ref[rows, :] = product
    rows = acc_ref[...].T
    core = lax.axis_index("core")

    @pl.when(core == 0)
    def _():
        out_ref[...] = rows

    @pl.when(core == 1)
    def _():
        for i in range(8):
            for z in range(8):
                source, dest = (i * 8 + z) * 4, (z * 8 + i) * 4
                out_ref[dest : dest + 4, :] = rows[source : source + 4, :]


def project(temps, area_weight, eofs):
    cols = temps.shape[1]
    blocks = cols // COL_BLOCK
    return pl.pallas_call(
        project_kernel,
        in_specs=[ANY_SPEC, ANY_SPEC, ANY_SPEC],
        out_specs=VMEM_SPEC,
        out_shape=pltpu.VMEM((CHANNELS, HOURS_DEV), jnp.float32),
        scratch_shapes=[
            pltpu.VMEM((blocks, HOURS_DEV, COL_BLOCK), jnp.float32),
            pltpu.VMEM((cols // 128, 128), jnp.float32),
            pltpu.VMEM((blocks, COL_BLOCK, CHANNELS), jnp.bfloat16),
            pltpu.VMEM((HOURS_DEV, CHANNELS), jnp.float32),
            pltpu.SemaphoreType.DMA((blocks,)),
            pltpu.SemaphoreType.DMA((blocks,)),
            pltpu.SemaphoreType.DMA(()),
        ],
        name="project",
    )(temps, area_weight.reshape(cols // 128, 128), eofs)


def sum_rows_kernel(parts_ref, out_ref):
    total = jnp.sum(parts_ref[...], axis=0)
    for owner in range(8):
        for seg in range(4):
            out_ref[owner, seg * 4 : seg * 4 + 4, :] = total[owner * 4 : owner * 4 + 4, seg * 128 : seg * 128 + 128]


def sum_rows(parts):
    return pl.pallas_call(
        sum_rows_kernel,
        in_specs=[VMEM_SPEC],
        out_specs=VMEM_SPEC,
        out_shape=pltpu.VMEM((8, 16, 128), jnp.float32),
        name="sum_rows",
    )(on_chip(parts))


def place(block, dest_ref):
    for source in range(16):
        chan, half = source // 2, source % 2
        for core in range(2):
            for seg in range(4):
                row = core * 16 + seg * 4
                hour = ((half * 2 + core) * 4 + seg) * 128
                dest_ref[chan * 4 : chan * 4 + 4, hour : hour + 128] = block[source, row : row + 4, :]


def split(x):
    high = x.astype(jnp.bfloat16)
    return high, (x - high.astype(jnp.float32)).astype(jnp.bfloat16)


def tiles_kernel(mine_ref, other_ref, out_ref, a_ref, b_ref, shifted_ref):
    core = lax.axis_index("core")
    first_lag = (lax.axis_index("xh") * 2 + core) * LAGS_DEV
    mine = mine_ref[...]
    other = other_ref[...]
    place(jnp.where(core == 0, mine, other), a_ref)
    place(jnp.where(core == 0, other, mine), b_ref)
    a = a_ref[...]
    a = a - jnp.sum(a, axis=1, keepdims=True) * (1.0 / HOURS)
    b = b_ref[:, :HOURS]
    b_ref[:, :HOURS] = b - jnp.sum(b, axis=1, keepdims=True) * (1.0 / HOURS)
    b_ref[:, HOURS:] = jnp.zeros((TILE, 128), jnp.float32)
    width = HOURS + 128
    ext = pltpu.roll(b_ref[...], jnp.where(first_lag == 0, 0, width - first_lag), 1)
    half = LAGS_DEV // 2
    late = jnp.where(lax.broadcasted_iota(jnp.int32, a.shape, 1) < half, 0.0, pltpu.roll(a, half, 1))
    left = jnp.concatenate([*split(a), *split(late)], axis=0)
    for lag in range(half):
        moved = (pltpu.roll(ext, width - lag, 1) if lag else ext)[:, :HOURS]
        high, low = split(moved)
        shifted_ref[lag * TILE : (lag + 1) * TILE, :] = high
        shifted_ref[128 + lag * TILE : 128 + (lag + 1) * TILE, :] = low
    product = lax.dot_general(
        left, shifted_ref[...], (((1,), (1,)), ((), ())), preferred_element_type=jnp.float32
    )
    for p in range(2):
        high, low = product[2 * p * TILE : (2 * p + 1) * TILE, :], product[(2 * p + 1) * TILE : (2 * p + 2) * TILE, :]
        tile = (high[:, :128] + low[:, :128] + high[:, 128:]) * (1.0 / HOURS)
        for owner in range(8):
            out_ref[owner, p * 4 : p * 4 + 4, :] = tile[owner * 4 : owner * 4 + 4, :]


def tiles(mine, other):
    return pl.pallas_call(
        tiles_kernel,
        in_specs=[VMEM_SPEC, VMEM_SPEC],
        out_specs=VMEM_SPEC,
        out_shape=pltpu.VMEM((8, 8, 128), jnp.float32),
        scratch_shapes=[
            pltpu.VMEM((TILE, HOURS), jnp.float32),
            pltpu.VMEM((TILE, HOURS + 128), jnp.float32),
            pltpu.VMEM((LAGS_DEV * TILE, HOURS), jnp.bfloat16),
        ],
        name="tiles",
    )(on_chip(mine), on_chip(other))


def spread_kernel(parts_ref, out_ref):
    for lag in range(LAGS_DEV):
        row, lane = 4 * (lag // 4), TILE * (lag % 4)
        for source in range(8):
            out_ref[lag, :, source * TILE : (source + 1) * TILE] = parts_ref[source, row : row + 4, lane : lane + TILE]


def spread(parts):
    return pl.pallas_call(
        spread_kernel,
        in_specs=[VMEM_SPEC],
        out_specs=VMEM_SPEC,
        out_shape=jax.ShapeDtypeStruct((LAGS_DEV, 4, CHANNELS), jnp.float32),
        name="spread",
    )(on_chip(parts))


def device(i, z, xh, core):
    return ((i * 8 + z) * 2 + xh) * 2 + core


PLANES = [[[device(i, z, xh, core) for i in range(8)] for z in range(8) for xh in range(2)] for core in range(2)]
LINES = [[[device(i, z, xh, core) for z in range(8)] for i in range(8) for xh in range(2)] for core in range(2)]
FIRST_GROUPS = PLANES[0] + LINES[1]
SECOND_GROUPS = LINES[0] + PLANES[1]
GATHER_GROUPS = [[device(i, z, xh, 0) for i in range(8) for xh in range(2)] for z in range(8)] + [
    [device(i, z, xh, 1) for z in range(8) for xh in range(2)] for i in range(8)
]
SWAP = [(0, 1), (1, 0)]


def shards(temps, area_weight, eofs):
    partial_sums = project(temps, area_weight, eofs)
    parts = lax.all_to_all(
        partial_sums.reshape(8, TILE, HOURS_DEV), AXES, 0, 0, axis_index_groups=FIRST_GROUPS
    )
    parts = lax.all_to_all(sum_rows(parts), AXES, 0, 0, axis_index_groups=SECOND_GROUPS)
    piece = jnp.sum(parts, axis=0)
    core = lax.axis_index("core")
    neighbour = lax.ppermute(piece, "core", SWAP)
    pair = jnp.where(
        core == 0,
        jnp.concatenate([piece, neighbour], axis=0),
        jnp.concatenate([neighbour, piece], axis=0),
    )
    mine = lax.all_to_all(
        jnp.broadcast_to(pair[None], (16, 32, 128)), AXES, 0, 0, axis_index_groups=GATHER_GROUPS
    )
    other = lax.ppermute(mine, "core", SWAP)
    out = lax.all_to_all(tiles(mine, other), ("xl", "y"), 0, 0)
    return spread(out)


def solution(mesh):
    fine = Mesh(mesh.devices.reshape(SIZES), AXES)
    grid, tm = ("xl", "y", "z"), ("xh", "core")
    return jax.shard_map(
        shards,
        mesh=fine,
        in_specs=(P(tm, grid), P(grid), P(grid, None)),
        out_specs=P(tm, grid, None),
        check_vma=False,
    )
```

```python
import jax
import jax.numpy as jnp
from jax import lax
from jax.experimental import pallas as pl
from jax.experimental.pallas import tpu as pltpu
from jax.sharding import Mesh, PartitionSpec as P

AXES = ("xl", "y", "z", "xh", "core")
SIZES = (2, 4, 8, 2, 2)
COL_BLOCK = 512
ROW_BLOCK = 256
COPIES_AHEAD = 4
HOURS = 2048
HOURS_DEV = 512
CHANNELS = 256
LAGS_DEV = 8
TILE = 32
LINE_ORDER = (4, 3, 2, 1, 0, 7, 6, 5)
PLANE_ORDER = (6, 5, 4, 7, 2, 1, 0, 3)
OUT_ORDER = (6, 5, 4, 7, 2, 1, 0, 3)
HALF_ORDER = (1, 0)
VMEM_SPEC = pl.BlockSpec(memory_space=pltpu.VMEM)
ANY_SPEC = pl.BlockSpec(memory_space=pl.ANY)


def on_chip(x):
    return pltpu.with_memory_space_constraint(x, pltpu.VMEM)


def project_kernel(temps_hbm, weight_hbm, eofs_hbm, out_ref, temps, weight, eofs, acc_ref, temps_sem, eofs_sem, weight_sem):
    blocks = temps.shape[0]
    weight_copy = pltpu.make_async_copy(weight_hbm, weight, weight_sem)
    weight_copy.start()
    temps_copies = [
        pltpu.make_async_copy(temps_hbm.at[:, pl.ds(k * COL_BLOCK, COL_BLOCK)], temps.at[k], temps_sem.at[k])
        for k in range(blocks)
    ]
    eofs_copies = [
        pltpu.make_async_copy(eofs_hbm.at[pl.ds(k * COL_BLOCK, COL_BLOCK), :], eofs.at[k], eofs_sem.at[k])
        for k in range(blocks)
    ]
    for k in range(COPIES_AHEAD):
        temps_copies[k].start()
        eofs_copies[k].start()
    weight_copy.wait()
    for k in range(blocks):
        temps_copies[k].wait()
        eofs_copies[k].wait()
        if k + COPIES_AHEAD < blocks:
            temps_copies[k + COPIES_AHEAD].start()
            eofs_copies[k + COPIES_AHEAD].start()
        first = k * (COL_BLOCK // 128)
        column_weight = jnp.concatenate(
            [weight[first + j : first + j + 1, :] for j in range(COL_BLOCK // 128)], axis=1
        )
        for row in range(0, HOURS_DEV, ROW_BLOCK):
            rows = slice(row, row + ROW_BLOCK)
            weighted = temps[k, rows, :] * column_weight
            high = weighted.astype(jnp.bfloat16)
            low = (weighted - high.astype(jnp.float32)).astype(jnp.bfloat16)
            product = jnp.dot(high, eofs[k], preferred_element_type=jnp.float32) + jnp.dot(
                low, eofs[k], preferred_element_type=jnp.float32
            )
            if k:
                acc_ref[rows, :] += product
            else:
                acc_ref[rows, :] = product
    rows = acc_ref[...].T
    core = lax.axis_index("core")

    @pl.when(core == 0)
    def _():
        for k, i in enumerate(PLANE_ORDER):
            for m, z in enumerate(LINE_ORDER):
                out_ref[k * 32 + m * 4 : k * 32 + m * 4 + 4, :] = rows[i * 32 + z * 4 : i * 32 + z * 4 + 4, :]

    @pl.when(core == 1)
    def _():
        for k, z in enumerate(LINE_ORDER):
            for m, i in enumerate(PLANE_ORDER):
                out_ref[k * 32 + m * 4 : k * 32 + m * 4 + 4, :] = rows[i * 32 + z * 4 : i * 32 + z * 4 + 4, :]


def project(temps, area_weight, eofs):
    cols = temps.shape[1]
    blocks = cols // COL_BLOCK
    return pl.pallas_call(
        project_kernel,
        in_specs=[ANY_SPEC, ANY_SPEC, ANY_SPEC],
        out_specs=VMEM_SPEC,
        out_shape=pltpu.VMEM((CHANNELS, HOURS_DEV), jnp.float32),
        scratch_shapes=[
            pltpu.VMEM((blocks, HOURS_DEV, COL_BLOCK), jnp.float32),
            pltpu.VMEM((cols // 128, 128), jnp.float32),
            pltpu.VMEM((blocks, COL_BLOCK, CHANNELS), jnp.bfloat16),
            pltpu.VMEM((HOURS_DEV, CHANNELS), jnp.float32),
            pltpu.SemaphoreType.DMA((blocks,)),
            pltpu.SemaphoreType.DMA((blocks,)),
            pltpu.SemaphoreType.DMA(()),
        ],
        name="project",
    )(temps, area_weight.reshape(cols // 128, 128), eofs)


def sum_rows_kernel(parts_ref, out_ref):
    total = jnp.sum(parts_ref[...], axis=0)
    for owner in range(8):
        for seg in range(4):
            out_ref[owner, seg * 4 : seg * 4 + 4, :] = total[owner * 4 : owner * 4 + 4, seg * 128 : seg * 128 + 128]


def sum_rows(parts):
    return pl.pallas_call(
        sum_rows_kernel,
        in_specs=[VMEM_SPEC],
        out_specs=VMEM_SPEC,
        out_shape=pltpu.VMEM((8, 16, 128), jnp.float32),
        name="sum_rows",
    )(on_chip(parts))


def place(block, dest_ref, order):
    for source in range(16):
        half, chan = HALF_ORDER[source // 8], order[source % 8]
        for core in range(2):
            for seg in range(4):
                row = core * 16 + seg * 4
                hour = ((half * 2 + core) * 4 + seg) * 128
                dest_ref[chan * 4 : chan * 4 + 4, hour : hour + 128] = block[source, row : row + 4, :]


def split(x):
    high = x.astype(jnp.bfloat16)
    return high, (x - high.astype(jnp.float32)).astype(jnp.bfloat16)


def tiles_kernel(mine_ref, other_ref, out_ref, a_ref, b_ref, shifted_ref):
    core = lax.axis_index("core")
    first_lag = (lax.axis_index("xh") * 2 + core) * LAGS_DEV
    mine = mine_ref[...]
    other = other_ref[...]
    place(jnp.where(core == 0, mine, other), a_ref, PLANE_ORDER)
    place(jnp.where(core == 0, other, mine), b_ref, LINE_ORDER)
    a = a_ref[...]
    a = a - jnp.sum(a, axis=1, keepdims=True) * (1.0 / HOURS)
    b = b_ref[:, :HOURS]
    b_ref[:, :HOURS] = b - jnp.sum(b, axis=1, keepdims=True) * (1.0 / HOURS)
    b_ref[:, HOURS:] = jnp.zeros((TILE, 128), jnp.float32)
    width = HOURS + 128
    ext = pltpu.roll(b_ref[...], jnp.where(first_lag == 0, 0, width - first_lag), 1)
    half = LAGS_DEV // 2
    late = jnp.where(lax.broadcasted_iota(jnp.int32, a.shape, 1) < half, 0.0, pltpu.roll(a, half, 1))
    left = jnp.concatenate([*split(a), *split(late)], axis=0)
    for lag in range(half):
        moved = (pltpu.roll(ext, width - lag, 1) if lag else ext)[:, :HOURS]
        high, low = split(moved)
        shifted_ref[lag * TILE : (lag + 1) * TILE, :] = high
        shifted_ref[128 + lag * TILE : 128 + (lag + 1) * TILE, :] = low
    product = lax.dot_general(
        left, shifted_ref[...], (((1,), (1,)), ((), ())), preferred_element_type=jnp.float32
    )
    for p in range(2):
        high, low = product[2 * p * TILE : (2 * p + 1) * TILE, :], product[(2 * p + 1) * TILE : (2 * p + 2) * TILE, :]
        tile = (high[:, :128] + low[:, :128] + high[:, 128:]) * (1.0 / HOURS)
        for k, owner in enumerate(OUT_ORDER):
            out_ref[k, p * 4 : p * 4 + 4, :] = tile[owner * 4 : owner * 4 + 4, :]


def tiles(mine, other):
    return pl.pallas_call(
        tiles_kernel,
        in_specs=[VMEM_SPEC, VMEM_SPEC],
        out_specs=VMEM_SPEC,
        out_shape=pltpu.VMEM((8, 8, 128), jnp.float32),
        scratch_shapes=[
            pltpu.VMEM((TILE, HOURS), jnp.float32),
            pltpu.VMEM((TILE, HOURS + 128), jnp.float32),
            pltpu.VMEM((LAGS_DEV * TILE, HOURS), jnp.bfloat16),
        ],
        name="tiles",
    )(on_chip(mine), on_chip(other))


def spread_kernel(parts_ref, out_ref):
    for lag in range(LAGS_DEV):
        row, lane = 4 * (lag // 4), TILE * (lag % 4)
        for k, source in enumerate(OUT_ORDER):
            out_ref[lag, :, source * TILE : (source + 1) * TILE] = parts_ref[k, row : row + 4, lane : lane + TILE]


def spread(parts):
    return pl.pallas_call(
        spread_kernel,
        in_specs=[VMEM_SPEC],
        out_specs=VMEM_SPEC,
        out_shape=jax.ShapeDtypeStruct((LAGS_DEV, 4, CHANNELS), jnp.float32),
        name="spread",
    )(on_chip(parts))


def device(i, z, xh, core):
    return ((i * 8 + z) * 2 + xh) * 2 + core


def planes(core, order):
    return [[device(i, z, xh, core) for i in order] for z in range(8) for xh in range(2)]


def lines(core):
    return [[device(i, z, xh, core) for z in LINE_ORDER] for i in range(8) for xh in range(2)]


FIRST_GROUPS = planes(0, PLANE_ORDER) + lines(1)
SECOND_GROUPS = lines(0) + planes(1, PLANE_ORDER)
GATHER_GROUPS = [[device(i, z, xh, 0) for xh in HALF_ORDER for i in PLANE_ORDER] for z in range(8)] + [
    [device(i, z, xh, 1) for xh in HALF_ORDER for z in LINE_ORDER] for i in range(8)
]
OUT_GROUPS = planes(0, OUT_ORDER) + planes(1, OUT_ORDER)
SWAP = [(0, 1), (1, 0)]


def shards(temps, area_weight, eofs):
    partial_sums = project(temps, area_weight, eofs)
    parts = lax.all_to_all(
        partial_sums.reshape(8, TILE, HOURS_DEV), AXES, 0, 0, axis_index_groups=FIRST_GROUPS
    )
    parts = lax.all_to_all(sum_rows(parts), AXES, 0, 0, axis_index_groups=SECOND_GROUPS)
    piece = jnp.sum(parts, axis=0)
    core = lax.axis_index("core")
    neighbour = lax.ppermute(piece, "core", SWAP)
    pair = jnp.where(
        core == 0,
        jnp.concatenate([piece, neighbour], axis=0),
        jnp.concatenate([neighbour, piece], axis=0),
    )
    mine = lax.all_to_all(
        jnp.broadcast_to(pair[None], (16, 32, 128)), AXES, 0, 0, axis_index_groups=GATHER_GROUPS
    )
    other = lax.ppermute(mine, "core", SWAP)
    out = lax.all_to_all(tiles(mine, other), AXES, 0, 0, axis_index_groups=OUT_GROUPS)
    return spread(out)


def solution(mesh):
    fine = Mesh(mesh.devices.reshape(SIZES), AXES)
    grid, tm = ("xl", "y", "z"), ("xh", "core")
    return jax.shard_map(
        shards,
        mesh=fine,
        in_specs=(P(tm, grid), P(grid), P(grid, None)),
        out_specs=P(tm, grid, None),
        check_vma=False,
    )
```

```python
import jax
import jax.numpy as jnp
from jax import lax
from jax.experimental import pallas as pl
from jax.experimental.pallas import tpu as pltpu
from jax.sharding import Mesh, PartitionSpec as P

AXES = ("xl", "y", "z", "xh", "core")
SIZES = (2, 4, 8, 2, 2)
COL_BLOCK = 512
ROW_BLOCK = 256
COPIES_AHEAD = 4
HOURS = 2048
HOURS_DEV = 512
CHANNELS = 256
LAGS_DEV = 8
TILE = 32
LINE_ORDER = (4, 3, 2, 1, 0, 7, 6, 5)
PLANE_ORDER = (6, 5, 4, 7, 2, 1, 0, 3)
OUT_ORDER = (6, 5, 4, 7, 2, 1, 0, 3)
HALF_ORDER = (1, 0)
VMEM_SPEC = pl.BlockSpec(memory_space=pltpu.VMEM)
ANY_SPEC = pl.BlockSpec(memory_space=pl.ANY)


def on_chip(x):
    return pltpu.with_memory_space_constraint(x, pltpu.VMEM)


def project_kernel(temps_hbm, weight_hbm, eofs_hbm, out_ref, temps, weight, eofs, acc_ref, temps_sem, eofs_sem, weight_sem):
    blocks = temps.shape[0]
    weight_copy = pltpu.make_async_copy(weight_hbm, weight, weight_sem)
    weight_copy.start()
    temps_copies = [
        pltpu.make_async_copy(temps_hbm.at[:, pl.ds(k * COL_BLOCK, COL_BLOCK)], temps.at[k], temps_sem.at[k])
        for k in range(blocks)
    ]
    eofs_copies = [
        pltpu.make_async_copy(eofs_hbm.at[pl.ds(k * COL_BLOCK, COL_BLOCK), :], eofs.at[k], eofs_sem.at[k])
        for k in range(blocks)
    ]
    for k in range(COPIES_AHEAD):
        temps_copies[k].start(priority=k % 2)
        eofs_copies[k].start()
    weight_copy.wait()
    for k in range(blocks):
        temps_copies[k].wait()
        eofs_copies[k].wait()
        if k + COPIES_AHEAD < blocks:
            temps_copies[k + COPIES_AHEAD].start(priority=k % 2)
            eofs_copies[k + COPIES_AHEAD].start()
        first = k * (COL_BLOCK // 128)
        column_weight = jnp.concatenate(
            [weight[first + j : first + j + 1, :] for j in range(COL_BLOCK // 128)], axis=1
        )
        for row in range(0, HOURS_DEV, ROW_BLOCK):
            rows = slice(row, row + ROW_BLOCK)
            weighted = temps[k, rows, :] * column_weight
            high = weighted.astype(jnp.bfloat16)
            low = (weighted - high.astype(jnp.float32)).astype(jnp.bfloat16)
            product = jnp.dot(high, eofs[k], preferred_element_type=jnp.float32) + jnp.dot(
                low, eofs[k], preferred_element_type=jnp.float32
            )
            if k:
                acc_ref[rows, :] += product
            else:
                acc_ref[rows, :] = product
    rows = acc_ref[...].T
    core = lax.axis_index("core")

    @pl.when(core == 0)
    def _():
        for k, i in enumerate(PLANE_ORDER):
            for m, z in enumerate(LINE_ORDER):
                out_ref[k * 32 + m * 4 : k * 32 + m * 4 + 4, :] = rows[i * 32 + z * 4 : i * 32 + z * 4 + 4, :]

    @pl.when(core == 1)
    def _():
        for k, z in enumerate(LINE_ORDER):
            for m, i in enumerate(PLANE_ORDER):
                out_ref[k * 32 + m * 4 : k * 32 + m * 4 + 4, :] = rows[i * 32 + z * 4 : i * 32 + z * 4 + 4, :]


def project(temps, area_weight, eofs):
    cols = temps.shape[1]
    blocks = cols // COL_BLOCK
    return pl.pallas_call(
        project_kernel,
        in_specs=[ANY_SPEC, ANY_SPEC, ANY_SPEC],
        out_specs=VMEM_SPEC,
        out_shape=pltpu.VMEM((CHANNELS, HOURS_DEV), jnp.float32),
        scratch_shapes=[
            pltpu.VMEM((blocks, HOURS_DEV, COL_BLOCK), jnp.float32),
            pltpu.VMEM((cols // 128, 128), jnp.float32),
            pltpu.VMEM((blocks, COL_BLOCK, CHANNELS), jnp.bfloat16),
            pltpu.VMEM((HOURS_DEV, CHANNELS), jnp.float32),
            pltpu.SemaphoreType.DMA((blocks,)),
            pltpu.SemaphoreType.DMA((blocks,)),
            pltpu.SemaphoreType.DMA(()),
        ],
        name="project",
    )(temps, area_weight.reshape(cols // 128, 128), eofs)


def sum_rows_kernel(parts_ref, out_ref):
    total = jnp.sum(parts_ref[...], axis=0)
    for owner in range(8):
        for seg in range(4):
            out_ref[owner, seg * 4 : seg * 4 + 4, :] = total[owner * 4 : owner * 4 + 4, seg * 128 : seg * 128 + 128]


def sum_rows(parts):
    return pl.pallas_call(
        sum_rows_kernel,
        in_specs=[VMEM_SPEC],
        out_specs=VMEM_SPEC,
        out_shape=pltpu.VMEM((8, 16, 128), jnp.float32),
        name="sum_rows",
    )(on_chip(parts))


def place(block, dest_ref, order):
    for source in range(16):
        half, chan = HALF_ORDER[source // 8], order[source % 8]
        for core in range(2):
            for seg in range(4):
                row = core * 16 + seg * 4
                hour = ((half * 2 + core) * 4 + seg) * 128
                dest_ref[chan * 4 : chan * 4 + 4, hour : hour + 128] = block[source, row : row + 4, :]


def split(x):
    high = x.astype(jnp.bfloat16)
    return high, (x - high.astype(jnp.float32)).astype(jnp.bfloat16)


def tiles_kernel(mine_ref, other_ref, out_ref, a_ref, b_ref, shifted_ref):
    core = lax.axis_index("core")
    first_lag = (lax.axis_index("xh") * 2 + core) * LAGS_DEV
    mine = mine_ref[...]
    other = other_ref[...]
    place(jnp.where(core == 0, mine, other), a_ref, PLANE_ORDER)
    place(jnp.where(core == 0, other, mine), b_ref, LINE_ORDER)
    a = a_ref[...]
    a = a - jnp.sum(a, axis=1, keepdims=True) * (1.0 / HOURS)
    b = b_ref[:, :HOURS]
    b_ref[:, :HOURS] = b - jnp.sum(b, axis=1, keepdims=True) * (1.0 / HOURS)
    b_ref[:, HOURS:] = jnp.zeros((TILE, 128), jnp.float32)
    width = HOURS + 128
    ext = pltpu.roll(b_ref[...], jnp.where(first_lag == 0, 0, width - first_lag), 1)
    half = LAGS_DEV // 2
    late = jnp.where(lax.broadcasted_iota(jnp.int32, a.shape, 1) < half, 0.0, pltpu.roll(a, half, 1))
    left = jnp.concatenate([*split(a), *split(late)], axis=0)
    for lag in range(half):
        moved = (pltpu.roll(ext, width - lag, 1) if lag else ext)[:, :HOURS]
        high, low = split(moved)
        shifted_ref[lag * TILE : (lag + 1) * TILE, :] = high
        shifted_ref[128 + lag * TILE : 128 + (lag + 1) * TILE, :] = low
    product = lax.dot_general(
        left, shifted_ref[...], (((1,), (1,)), ((), ())), preferred_element_type=jnp.float32
    )
    for p in range(2):
        high, low = product[2 * p * TILE : (2 * p + 1) * TILE, :], product[(2 * p + 1) * TILE : (2 * p + 2) * TILE, :]
        tile = (high[:, :128] + low[:, :128] + high[:, 128:]) * (1.0 / HOURS)
        for k, owner in enumerate(OUT_ORDER):
            out_ref[k, p * 4 : p * 4 + 4, :] = tile[owner * 4 : owner * 4 + 4, :]


def tiles(mine, other):
    return pl.pallas_call(
        tiles_kernel,
        in_specs=[VMEM_SPEC, VMEM_SPEC],
        out_specs=VMEM_SPEC,
        out_shape=pltpu.VMEM((8, 8, 128), jnp.float32),
        scratch_shapes=[
            pltpu.VMEM((TILE, HOURS), jnp.float32),
            pltpu.VMEM((TILE, HOURS + 128), jnp.float32),
            pltpu.VMEM((LAGS_DEV * TILE, HOURS), jnp.bfloat16),
        ],
        name="tiles",
    )(on_chip(mine), on_chip(other))


def spread_kernel(parts_ref, out_ref):
    for lag in range(LAGS_DEV):
        row, lane = 4 * (lag // 4), TILE * (lag % 4)
        for k, source in enumerate(OUT_ORDER):
            out_ref[lag, :, source * TILE : (source + 1) * TILE] = parts_ref[k, row : row + 4, lane : lane + TILE]


def spread(parts):
    return pl.pallas_call(
        spread_kernel,
        in_specs=[VMEM_SPEC],
        out_specs=VMEM_SPEC,
        out_shape=jax.ShapeDtypeStruct((LAGS_DEV, 4, CHANNELS), jnp.float32),
        name="spread",
    )(on_chip(parts))


def device(i, z, xh, core):
    return ((i * 8 + z) * 2 + xh) * 2 + core


def planes(core, order):
    return [[device(i, z, xh, core) for i in order] for z in range(8) for xh in range(2)]


def lines(core):
    return [[device(i, z, xh, core) for z in LINE_ORDER] for i in range(8) for xh in range(2)]


FIRST_GROUPS = planes(0, PLANE_ORDER) + lines(1)
SECOND_GROUPS = lines(0) + planes(1, PLANE_ORDER)
GATHER_GROUPS = [[device(i, z, xh, 0) for xh in HALF_ORDER for i in PLANE_ORDER] for z in range(8)] + [
    [device(i, z, xh, 1) for xh in HALF_ORDER for z in LINE_ORDER] for i in range(8)
]
OUT_GROUPS = planes(0, OUT_ORDER) + planes(1, OUT_ORDER)
SWAP = [(0, 1), (1, 0)]


def shards(temps, area_weight, eofs):
    partial_sums = project(temps, area_weight, eofs)
    parts = lax.all_to_all(
        partial_sums.reshape(8, TILE, HOURS_DEV), AXES, 0, 0, axis_index_groups=FIRST_GROUPS
    )
    parts = lax.all_to_all(sum_rows(parts), AXES, 0, 0, axis_index_groups=SECOND_GROUPS)
    piece = jnp.sum(parts, axis=0)
    core = lax.axis_index("core")
    neighbour = lax.ppermute(piece, "core", SWAP)
    pair = jnp.where(
        core == 0,
        jnp.concatenate([piece, neighbour], axis=0),
        jnp.concatenate([neighbour, piece], axis=0),
    )
    mine = lax.all_to_all(
        jnp.broadcast_to(pair[None], (16, 32, 128)), AXES, 0, 0, axis_index_groups=GATHER_GROUPS
    )
    other = lax.ppermute(mine, "core", SWAP)
    out = lax.all_to_all(tiles(mine, other), AXES, 0, 0, axis_index_groups=OUT_GROUPS)
    return spread(out)


def solution(mesh):
    fine = Mesh(mesh.devices.reshape(SIZES), AXES)
    grid, tm = ("xl", "y", "z"), ("xh", "core")
    return jax.shard_map(
        shards,
        mesh=fine,
        in_specs=(P(tm, grid), P(grid), P(grid, None)),
        out_specs=P(tm, grid, None),
        check_vma=False,
    )
```

```python
import jax
import jax.numpy as jnp
from jax import lax
from jax.experimental import pallas as pl
from jax.experimental.pallas import tpu as pltpu
from jax.sharding import Mesh, PartitionSpec as P

AXES = ("xl", "y", "z", "xh", "core")
SIZES = (2, 4, 8, 2, 2)
COL_BLOCK = 512
ROW_BLOCK = 256
COPIES_AHEAD = 4
HOURS = 2048
HOURS_DEV = 512
CHANNELS = 256
LAGS_DEV = 8
TILE = 32
LINE_ORDER = (4, 0, 3, 7, 2, 6, 1, 5)
PLANE_ORDER = (6, 0, 5, 3, 4, 2, 7, 1)
OUT_ORDER = (6, 0, 5, 3, 4, 2, 7, 1)
HALF_ORDER = (1, 0)
VMEM_SPEC = pl.BlockSpec(memory_space=pltpu.VMEM)
ANY_SPEC = pl.BlockSpec(memory_space=pl.ANY)


def on_chip(x):
    return pltpu.with_memory_space_constraint(x, pltpu.VMEM)


def project_kernel(temps_hbm, weight_hbm, eofs_hbm, out_ref, temps, weight, eofs, acc_ref, temps_sem, eofs_sem, weight_sem):
    blocks = temps.shape[0]
    weight_copy = pltpu.make_async_copy(weight_hbm, weight, weight_sem)
    weight_copy.start()
    temps_copies = [
        pltpu.make_async_copy(temps_hbm.at[:, pl.ds(k * COL_BLOCK, COL_BLOCK)], temps.at[k], temps_sem.at[k])
        for k in range(blocks)
    ]
    eofs_copies = [
        pltpu.make_async_copy(eofs_hbm.at[pl.ds(k * COL_BLOCK, COL_BLOCK), :], eofs.at[k], eofs_sem.at[k])
        for k in range(blocks)
    ]
    for k in range(COPIES_AHEAD):
        temps_copies[k].start(priority=k % 2)
        eofs_copies[k].start()
    weight_copy.wait()
    for k in range(blocks):
        temps_copies[k].wait()
        eofs_copies[k].wait()
        if k + COPIES_AHEAD < blocks:
            temps_copies[k + COPIES_AHEAD].start(priority=k % 2)
            eofs_copies[k + COPIES_AHEAD].start()
        first = k * (COL_BLOCK // 128)
        column_weight = jnp.concatenate(
            [weight[first + j : first + j + 1, :] for j in range(COL_BLOCK // 128)], axis=1
        )
        for row in range(0, HOURS_DEV, ROW_BLOCK):
            rows = slice(row, row + ROW_BLOCK)
            weighted = temps[k, rows, :] * column_weight
            high = weighted.astype(jnp.bfloat16)
            low = (weighted - high.astype(jnp.float32)).astype(jnp.bfloat16)
            product = jnp.dot(high, eofs[k], preferred_element_type=jnp.float32) + jnp.dot(
                low, eofs[k], preferred_element_type=jnp.float32
            )
            if k:
                acc_ref[rows, :] += product
            else:
                acc_ref[rows, :] = product
    rows = acc_ref[...].T
    core = lax.axis_index("core")

    @pl.when(core == 0)
    def _():
        for k, i in enumerate(PLANE_ORDER):
            for m, z in enumerate(LINE_ORDER):
                out_ref[k * 32 + m * 4 : k * 32 + m * 4 + 4, :] = rows[i * 32 + z * 4 : i * 32 + z * 4 + 4, :]

    @pl.when(core == 1)
    def _():
        for k, z in enumerate(LINE_ORDER):
            for m, i in enumerate(PLANE_ORDER):
                out_ref[k * 32 + m * 4 : k * 32 + m * 4 + 4, :] = rows[i * 32 + z * 4 : i * 32 + z * 4 + 4, :]


def project(temps, area_weight, eofs):
    cols = temps.shape[1]
    blocks = cols // COL_BLOCK
    return pl.pallas_call(
        project_kernel,
        in_specs=[ANY_SPEC, ANY_SPEC, ANY_SPEC],
        out_specs=VMEM_SPEC,
        out_shape=pltpu.VMEM((CHANNELS, HOURS_DEV), jnp.float32),
        scratch_shapes=[
            pltpu.VMEM((blocks, HOURS_DEV, COL_BLOCK), jnp.float32),
            pltpu.VMEM((cols // 128, 128), jnp.float32),
            pltpu.VMEM((blocks, COL_BLOCK, CHANNELS), jnp.bfloat16),
            pltpu.VMEM((HOURS_DEV, CHANNELS), jnp.float32),
            pltpu.SemaphoreType.DMA((blocks,)),
            pltpu.SemaphoreType.DMA((blocks,)),
            pltpu.SemaphoreType.DMA(()),
        ],
        name="project",
    )(temps, area_weight.reshape(cols // 128, 128), eofs)


def sum_rows_kernel(parts_ref, out_ref):
    total = jnp.sum(parts_ref[...], axis=0)
    for owner in range(8):
        for seg in range(4):
            out_ref[owner, seg * 4 : seg * 4 + 4, :] = total[owner * 4 : owner * 4 + 4, seg * 128 : seg * 128 + 128]


def sum_rows(parts):
    return pl.pallas_call(
        sum_rows_kernel,
        in_specs=[VMEM_SPEC],
        out_specs=VMEM_SPEC,
        out_shape=pltpu.VMEM((8, 16, 128), jnp.float32),
        name="sum_rows",
    )(on_chip(parts))


def place(block, dest_ref, order):
    for source in range(16):
        half, chan = HALF_ORDER[source // 8], order[source % 8]
        for core in range(2):
            for seg in range(4):
                row = core * 16 + seg * 4
                hour = ((half * 2 + core) * 4 + seg) * 128
                dest_ref[chan * 4 : chan * 4 + 4, hour : hour + 128] = block[source, row : row + 4, :]


def split(x):
    high = x.astype(jnp.bfloat16)
    return high, (x - high.astype(jnp.float32)).astype(jnp.bfloat16)


def tiles_kernel(mine_ref, other_ref, out_ref, a_ref, b_ref, shifted_ref):
    core = lax.axis_index("core")
    first_lag = (lax.axis_index("xh") * 2 + core) * LAGS_DEV
    mine = mine_ref[...]
    other = other_ref[...]
    place(jnp.where(core == 0, mine, other), a_ref, PLANE_ORDER)
    place(jnp.where(core == 0, other, mine), b_ref, LINE_ORDER)
    a = a_ref[...]
    a = a - jnp.sum(a, axis=1, keepdims=True) * (1.0 / HOURS)
    b = b_ref[:, :HOURS]
    b_ref[:, :HOURS] = b - jnp.sum(b, axis=1, keepdims=True) * (1.0 / HOURS)
    b_ref[:, HOURS:] = jnp.zeros((TILE, 128), jnp.float32)
    width = HOURS + 128
    ext = pltpu.roll(b_ref[...], jnp.where(first_lag == 0, 0, width - first_lag), 1)
    half = LAGS_DEV // 2
    late = jnp.where(lax.broadcasted_iota(jnp.int32, a.shape, 1) < half, 0.0, pltpu.roll(a, half, 1))
    left = jnp.concatenate([*split(a), *split(late)], axis=0)
    for lag in range(half):
        moved = (pltpu.roll(ext, width - lag, 1) if lag else ext)[:, :HOURS]
        high, low = split(moved)
        shifted_ref[lag * TILE : (lag + 1) * TILE, :] = high
        shifted_ref[128 + lag * TILE : 128 + (lag + 1) * TILE, :] = low
    product = lax.dot_general(
        left, shifted_ref[...], (((1,), (1,)), ((), ())), preferred_element_type=jnp.float32
    )
    for p in range(2):
        high, low = product[2 * p * TILE : (2 * p + 1) * TILE, :], product[(2 * p + 1) * TILE : (2 * p + 2) * TILE, :]
        tile = (high[:, :128] + low[:, :128] + high[:, 128:]) * (1.0 / HOURS)
        for k, owner in enumerate(OUT_ORDER):
            out_ref[k, p * 4 : p * 4 + 4, :] = tile[owner * 4 : owner * 4 + 4, :]


def tiles(mine, other):
    return pl.pallas_call(
        tiles_kernel,
        in_specs=[VMEM_SPEC, VMEM_SPEC],
        out_specs=VMEM_SPEC,
        out_shape=pltpu.VMEM((8, 8, 128), jnp.float32),
        scratch_shapes=[
            pltpu.VMEM((TILE, HOURS), jnp.float32),
            pltpu.VMEM((TILE, HOURS + 128), jnp.float32),
            pltpu.VMEM((LAGS_DEV * TILE, HOURS), jnp.bfloat16),
        ],
        name="tiles",
    )(on_chip(mine), on_chip(other))


def spread_kernel(parts_ref, out_ref):
    for lag in range(LAGS_DEV):
        row, lane = 4 * (lag // 4), TILE * (lag % 4)
        for k, source in enumerate(OUT_ORDER):
            out_ref[lag, :, source * TILE : (source + 1) * TILE] = parts_ref[k, row : row + 4, lane : lane + TILE]


def spread(parts):
    return pl.pallas_call(
        spread_kernel,
        in_specs=[VMEM_SPEC],
        out_specs=VMEM_SPEC,
        out_shape=jax.ShapeDtypeStruct((LAGS_DEV, 4, CHANNELS), jnp.float32),
        name="spread",
    )(on_chip(parts))


def device(i, z, xh, core):
    return ((i * 8 + z) * 2 + xh) * 2 + core


def planes(core, order):
    return [[device(i, z, xh, core) for i in order] for z in range(8) for xh in range(2)]


def lines(core):
    return [[device(i, z, xh, core) for z in LINE_ORDER] for i in range(8) for xh in range(2)]


FIRST_GROUPS = planes(0, PLANE_ORDER) + lines(1)
SECOND_GROUPS = lines(0) + planes(1, PLANE_ORDER)
GATHER_GROUPS = [[device(i, z, xh, 0) for xh in HALF_ORDER for i in PLANE_ORDER] for z in range(8)] + [
    [device(i, z, xh, 1) for xh in HALF_ORDER for z in LINE_ORDER] for i in range(8)
]
OUT_GROUPS = planes(0, OUT_ORDER) + planes(1, OUT_ORDER)
SWAP = [(0, 1), (1, 0)]


def shards(temps, area_weight, eofs):
    partial_sums = project(temps, area_weight, eofs)
    parts = lax.all_to_all(
        partial_sums.reshape(8, TILE, HOURS_DEV), AXES, 0, 0, axis_index_groups=FIRST_GROUPS
    )
    parts = lax.all_to_all(sum_rows(parts), AXES, 0, 0, axis_index_groups=SECOND_GROUPS)
    piece = jnp.sum(parts, axis=0)
    core = lax.axis_index("core")
    neighbour = lax.ppermute(piece, "core", SWAP)
    pair = jnp.where(
        core == 0,
        jnp.concatenate([piece, neighbour], axis=0),
        jnp.concatenate([neighbour, piece], axis=0),
    )
    mine = lax.all_to_all(
        jnp.broadcast_to(pair[None], (16, 32, 128)), AXES, 0, 0, axis_index_groups=GATHER_GROUPS
    )
    other = lax.ppermute(mine, "core", SWAP)
    out = lax.all_to_all(tiles(mine, other), AXES, 0, 0, axis_index_groups=OUT_GROUPS)
    return spread(out)


def solution(mesh):
    fine = Mesh(mesh.devices.reshape(SIZES), AXES)
    grid, tm = ("xl", "y", "z"), ("xh", "core")
    return jax.shard_map(
        shards,
        mesh=fine,
        in_specs=(P(tm, grid), P(grid), P(grid, None)),
        out_specs=P(tm, grid, None),
        check_vma=False,
    )
```

```python
import jax
import jax.numpy as jnp
from jax import lax
from jax.experimental import pallas as pl
from jax.experimental.pallas import tpu as pltpu
from jax.sharding import Mesh, PartitionSpec as P

AXES = ("xl", "y", "z", "xh", "core")
SIZES = (2, 4, 8, 2, 2)
COL_BLOCK = 512
ROW_BLOCK = 256
COPIES_AHEAD = 4
HOURS = 2048
HOURS_DEV = 512
CHANNELS = 256
LAGS_DEV = 8
TILE = 32
LINE_ORDER = (4, 0, 3, 7, 2, 6, 1, 5)
PLANE_ORDER = (6, 0, 5, 3, 4, 2, 7, 1)
OUT_ORDER = (6, 0, 5, 3, 4, 2, 7, 1)
HALF_ORDER = (1, 0)
VMEM_SPEC = pl.BlockSpec(memory_space=pltpu.VMEM)
ANY_SPEC = pl.BlockSpec(memory_space=pl.ANY)


def on_chip(x):
    return pltpu.with_memory_space_constraint(x, pltpu.VMEM)


def project_kernel(temps_hbm, weight_hbm, eofs_hbm, out_ref, temps, weight, eofs, acc_ref, temps_sem, eofs_sem, weight_sem):
    blocks = temps.shape[0]
    weight_copy = pltpu.make_async_copy(weight_hbm, weight, weight_sem)
    weight_copy.start()
    temps_copies = [
        pltpu.make_async_copy(temps_hbm.at[:, pl.ds(k * COL_BLOCK, COL_BLOCK)], temps.at[k], temps_sem.at[k])
        for k in range(blocks)
    ]
    eofs_copies = [
        pltpu.make_async_copy(eofs_hbm.at[pl.ds(k * 2 * COL_BLOCK, 2 * COL_BLOCK), :], eofs.at[k], eofs_sem.at[k])
        for k in range(blocks // 2)
    ]
    for k in range(COPIES_AHEAD):
        temps_copies[k].start(priority=k % 2)
        if k % 2 == 0:
            eofs_copies[k // 2].start()
    weight_copy.wait()
    for k in range(blocks):
        temps_copies[k].wait()
        if k % 2 == 0:
            eofs_copies[k // 2].wait()
        if k + COPIES_AHEAD < blocks:
            temps_copies[k + COPIES_AHEAD].start(priority=k % 2)
            if k % 2 == 0:
                eofs_copies[(k + COPIES_AHEAD) // 2].start()
        first = k * (COL_BLOCK // 128)
        block_eofs = eofs[k // 2, (k % 2) * COL_BLOCK : (k % 2 + 1) * COL_BLOCK, :]
        column_weight = jnp.concatenate(
            [weight[first + j : first + j + 1, :] for j in range(COL_BLOCK // 128)], axis=1
        )
        for row in range(0, HOURS_DEV, ROW_BLOCK):
            rows = slice(row, row + ROW_BLOCK)
            weighted = temps[k, rows, :] * column_weight
            high = weighted.astype(jnp.bfloat16)
            low = (weighted - high.astype(jnp.float32)).astype(jnp.bfloat16)
            product = jnp.dot(high, block_eofs, preferred_element_type=jnp.float32) + jnp.dot(
                low, block_eofs, preferred_element_type=jnp.float32
            )
            if k:
                acc_ref[rows, :] += product
            else:
                acc_ref[rows, :] = product
    rows = acc_ref[...].T
    core = lax.axis_index("core")

    @pl.when(core == 0)
    def _():
        for k, i in enumerate(PLANE_ORDER):
            for m, z in enumerate(LINE_ORDER):
                out_ref[k * 32 + m * 4 : k * 32 + m * 4 + 4, :] = rows[i * 32 + z * 4 : i * 32 + z * 4 + 4, :]

    @pl.when(core == 1)
    def _():
        for k, z in enumerate(LINE_ORDER):
            for m, i in enumerate(PLANE_ORDER):
                out_ref[k * 32 + m * 4 : k * 32 + m * 4 + 4, :] = rows[i * 32 + z * 4 : i * 32 + z * 4 + 4, :]


def project(temps, area_weight, eofs):
    cols = temps.shape[1]
    blocks = cols // COL_BLOCK
    return pl.pallas_call(
        project_kernel,
        in_specs=[ANY_SPEC, ANY_SPEC, ANY_SPEC],
        out_specs=VMEM_SPEC,
        out_shape=pltpu.VMEM((CHANNELS, HOURS_DEV), jnp.float32),
        scratch_shapes=[
            pltpu.VMEM((blocks, HOURS_DEV, COL_BLOCK), jnp.float32),
            pltpu.VMEM((cols // 128, 128), jnp.float32),
            pltpu.VMEM((blocks // 2, 2 * COL_BLOCK, CHANNELS), jnp.bfloat16),
            pltpu.VMEM((HOURS_DEV, CHANNELS), jnp.float32),
            pltpu.SemaphoreType.DMA((blocks,)),
            pltpu.SemaphoreType.DMA((blocks // 2,)),
            pltpu.SemaphoreType.DMA(()),
        ],
        name="project",
    )(temps, area_weight.reshape(cols // 128, 128), eofs)


def sum_rows_kernel(parts_ref, out_ref):
    total = jnp.sum(parts_ref[...], axis=0)
    for owner in range(8):
        for seg in range(4):
            out_ref[owner, seg * 4 : seg * 4 + 4, :] = total[owner * 4 : owner * 4 + 4, seg * 128 : seg * 128 + 128]


def sum_rows(parts):
    return pl.pallas_call(
        sum_rows_kernel,
        in_specs=[VMEM_SPEC],
        out_specs=VMEM_SPEC,
        out_shape=pltpu.VMEM((8, 16, 128), jnp.float32),
        name="sum_rows",
    )(on_chip(parts))


def place(block, dest_ref, order):
    for source in range(16):
        half, chan = HALF_ORDER[source // 8], order[source % 8]
        for core in range(2):
            for seg in range(4):
                row = core * 16 + seg * 4
                hour = ((half * 2 + core) * 4 + seg) * 128
                dest_ref[chan * 4 : chan * 4 + 4, hour : hour + 128] = block[source, row : row + 4, :]


def split(x):
    high = x.astype(jnp.bfloat16)
    return high, (x - high.astype(jnp.float32)).astype(jnp.bfloat16)


def tiles_kernel(mine_ref, other_ref, out_ref, a_ref, b_ref, shifted_ref):
    core = lax.axis_index("core")
    first_lag = (lax.axis_index("xh") * 2 + core) * LAGS_DEV
    mine = mine_ref[...]
    other = other_ref[...]
    place(jnp.where(core == 0, mine, other), a_ref, PLANE_ORDER)
    place(jnp.where(core == 0, other, mine), b_ref, LINE_ORDER)
    a = a_ref[...]
    a = a - jnp.sum(a, axis=1, keepdims=True) * (1.0 / HOURS)
    b = b_ref[:, :HOURS]
    b_ref[:, :HOURS] = b - jnp.sum(b, axis=1, keepdims=True) * (1.0 / HOURS)
    b_ref[:, HOURS:] = jnp.zeros((TILE, 128), jnp.float32)
    width = HOURS + 128
    ext = pltpu.roll(b_ref[...], jnp.where(first_lag == 0, 0, width - first_lag), 1)
    half = LAGS_DEV // 2
    late = jnp.where(lax.broadcasted_iota(jnp.int32, a.shape, 1) < half, 0.0, pltpu.roll(a, half, 1))
    left = jnp.concatenate([*split(a), *split(late)], axis=0)
    for lag in range(half):
        moved = (pltpu.roll(ext, width - lag, 1) if lag else ext)[:, :HOURS]
        high, low = split(moved)
        shifted_ref[lag * TILE : (lag + 1) * TILE, :] = high
        shifted_ref[128 + lag * TILE : 128 + (lag + 1) * TILE, :] = low
    product = lax.dot_general(
        left, shifted_ref[...], (((1,), (1,)), ((), ())), preferred_element_type=jnp.float32
    )
    for p in range(2):
        high, low = product[2 * p * TILE : (2 * p + 1) * TILE, :], product[(2 * p + 1) * TILE : (2 * p + 2) * TILE, :]
        tile = (high[:, :128] + low[:, :128] + high[:, 128:]) * (1.0 / HOURS)
        for k, owner in enumerate(OUT_ORDER):
            out_ref[k, p * 4 : p * 4 + 4, :] = tile[owner * 4 : owner * 4 + 4, :]


def tiles(mine, other):
    return pl.pallas_call(
        tiles_kernel,
        in_specs=[VMEM_SPEC, VMEM_SPEC],
        out_specs=VMEM_SPEC,
        out_shape=pltpu.VMEM((8, 8, 128), jnp.float32),
        scratch_shapes=[
            pltpu.VMEM((TILE, HOURS), jnp.float32),
            pltpu.VMEM((TILE, HOURS + 128), jnp.float32),
            pltpu.VMEM((LAGS_DEV * TILE, HOURS), jnp.bfloat16),
        ],
        name="tiles",
    )(on_chip(mine), on_chip(other))


def spread_kernel(parts_ref, out_ref):
    for lag in range(LAGS_DEV):
        row, lane = 4 * (lag // 4), TILE * (lag % 4)
        for k, source in enumerate(OUT_ORDER):
            out_ref[lag, :, source * TILE : (source + 1) * TILE] = parts_ref[k, row : row + 4, lane : lane + TILE]


def spread(parts):
    return pl.pallas_call(
        spread_kernel,
        in_specs=[VMEM_SPEC],
        out_specs=VMEM_SPEC,
        out_shape=jax.ShapeDtypeStruct((LAGS_DEV, 4, CHANNELS), jnp.float32),
        name="spread",
    )(on_chip(parts))


def device(i, z, xh, core):
    return ((i * 8 + z) * 2 + xh) * 2 + core


def planes(core, order):
    return [[device(i, z, xh, core) for i in order] for z in range(8) for xh in range(2)]


def lines(core):
    return [[device(i, z, xh, core) for z in LINE_ORDER] for i in range(8) for xh in range(2)]


FIRST_GROUPS = planes(0, PLANE_ORDER) + lines(1)
SECOND_GROUPS = lines(0) + planes(1, PLANE_ORDER)
GATHER_GROUPS = [[device(i, z, xh, 0) for xh in HALF_ORDER for i in PLANE_ORDER] for z in range(8)] + [
    [device(i, z, xh, 1) for xh in HALF_ORDER for z in LINE_ORDER] for i in range(8)
]
OUT_GROUPS = planes(0, OUT_ORDER) + planes(1, OUT_ORDER)
SWAP = [(0, 1), (1, 0)]


def shards(temps, area_weight, eofs):
    partial_sums = project(temps, area_weight, eofs)
    parts = lax.all_to_all(
        partial_sums.reshape(8, TILE, HOURS_DEV), AXES, 0, 0, axis_index_groups=FIRST_GROUPS
    )
    parts = lax.all_to_all(sum_rows(parts), AXES, 0, 0, axis_index_groups=SECOND_GROUPS)
    piece = jnp.sum(parts, axis=0)
    core = lax.axis_index("core")
    neighbour = lax.ppermute(piece, "core", SWAP)
    pair = jnp.where(
        core == 0,
        jnp.concatenate([piece, neighbour], axis=0),
        jnp.concatenate([neighbour, piece], axis=0),
    )
    mine = lax.all_to_all(
        jnp.broadcast_to(pair[None], (16, 32, 128)), AXES, 0, 0, axis_index_groups=GATHER_GROUPS
    )
    other = lax.ppermute(mine, "core", SWAP)
    out = lax.all_to_all(tiles(mine, other), AXES, 0, 0, axis_index_groups=OUT_GROUPS)
    return spread(out)


def solution(mesh):
    fine = Mesh(mesh.devices.reshape(SIZES), AXES)
    grid, tm = ("xl", "y", "z"), ("xh", "core")
    return jax.shard_map(
        shards,
        mesh=fine,
        in_specs=(P(tm, grid), P(grid), P(grid, None)),
        out_specs=P(tm, grid, None),
        check_vma=False,
    )
```
